256 devices in a mesh: cfg: 2 (over x_lo), seq: 32 (over x_hi, z, core), tp: 4 (over y).
Axes of the slice: x: 4 (x_hi: 2, x_lo: 2; x = x_hi * 2 + x_lo), y: 4, z: 8, core: 2. Of those that a mesh axis runs over, the one named last changes fastest.
Arguments:
- image: bfloat16 [16384, 3072], P('seq', 'tp'), may hold values from -6 to 6
- text: bfloat16 [2, 8192, 3072], P('cfg', 'seq', 'tp'), may hold values from -6 to 6
- modulation: float32 [2, 16, 3, 3072], P('cfg'), may hold values from -3 to 3
- w_qkv: bfloat16 [3072, 4608], P('seq', 'tp'), may hold values from -0.109375 to 0.109375
- q_gain: float32 [128], replicated, may hold values from 0.5 to 12, as said below
- k_gain: float32 [128], replicated, may hold values from 0.5 to 12, as said below
- w_proj: bfloat16 [1536, 3072], P('tp', 'seq'), may hold values from -0.15625 to 0.15625
- text_len: int32 [2, 16], replicated, may hold values from 1 to 512
- text_tiles: int32 [2, 16, 4], replicated, may hold values from 0 to 3, each once within a row
- step_index: int32 [16], replicated, may hold values from 0 to 27
Outputs:
- guided: float32 [16384, 3072], P('seq', ('cfg', 'tp'))
- latent_next: float32 [16384, 3072], P('seq', ('cfg', 'tp'))
The draws below stay inside these ranges and needn't reach their ends.
Inputs may be any that keep to these rules, and one draw needn't show every extreme that they name: `q_gain`: each query and key norm gain is positive. `k_gain`: each query and key norm gain is positive. `text_tiles`: each row of four is an order of 0 to 3.
All inputs are finite; a program needn't handle non-finite values.
Results may differ from the reference program's by a relative error of at most 0.015.
The reference program's roundings to bfloat16 on the way count: a program that leaves them out, or rounds other values in their place, can miss the bound.
Values may be sent and summed in bfloat16 or wider, within the bound.
No kernel may reach another device: no remote copies, remote signals or barrier semaphores. Data moves between devices by JAX's collectives and lax.ppermute only.
A program may use at most 128 MiB of HBM per device.

```python
import jax
import jax.numpy as jnp
from jax import lax

D = 3072
HEADS = 12
HD = 128
IMG = 1024
TXT = 512
STEPS = 28
PROMPTS = 16
IMGTOK = 16384
TXTTOK = 8192


def gain_draw(key):
    lower_end, upper_end = (0.5, 4.0)
    uniform_part = jax.random.uniform(key, (HD,), jnp.float32)
    return jnp.exp(jnp.log(lower_end) + uniform_part * (jnp.log(upper_end) - jnp.log(lower_end)))


def draw_q_gain(key, part):
    return gain_draw(jax.random.fold_in(key, 11))


def draw_k_gain(key, part):
    return gain_draw(jax.random.fold_in(key, 23))


def with_ends(array, rng, smallest, top_value):
    longest = array.shape.index(max(array.shape))
    spots = []
    for shift in (0, 1):
        where = [jax.random.randint(jax.random.fold_in(rng, axis), (), 0, length) for axis, length in enumerate(array.shape)]
        where[longest] = (where[longest] + shift) % array.shape[longest]
        spots.append(tuple(where))
    return array.at[spots[0]].set(smallest).at[spots[1]].set(top_value)


def block_levels(rng, shape, pieces, low, top_value):
    gain, own = 1.0, jax.random.fold_in(rng, 6)
    for dim, parts in pieces:
        steps = jnp.exp(jax.random.uniform(jax.random.fold_in(own, dim), (parts,), jnp.float32, low / len(pieces), top_value / len(pieces)))
        gain = gain * jnp.repeat(steps, shape[dim] // parts).reshape([-1 if axis == dim else 1 for axis in range(len(shape))])
    return gain


def gaussian(stream_key, shape, deviation, most, cuts=(), kind=jnp.bfloat16):
    entries = jax.random.normal(stream_key, shape, jnp.float32) * deviation
    if len(cuts) > 0:
        entries = block_levels(stream_key, shape, cuts, -0.22, 0.18) * entries
    return jnp.clip(entries, min=-most, max=most).astype(kind)


def setup_inputs(seed: int = 0) -> dict:
    key_of = jax.random.split(jax.random.key(seed), 11)
    return {
        "image": gaussian(key_of[0], (IMGTOK, D), 1.0, 6.0, ((0, 32), (1, 4))),
        "text": gaussian(key_of[1], (2, TXTTOK, D), 1.0, 6.0, ((0, 2), (1, 32), (2, 4))),
        "modulation": gaussian(key_of[2], (2, PROMPTS, 3, D), 0.5, 3.0, ((0, 2),), jnp.float32),
        "w_qkv": gaussian(key_of[3], (D, 3 * HEADS * HD), D ** -0.5, 0.109375, ((0, 32), (1, 4))),
        "q_gain": draw_q_gain(jax.random.fold_in(key_of[10], 71), 0),
        "k_gain": draw_k_gain(jax.random.fold_in(key_of[10], 71), 0),
        "w_proj": gaussian(key_of[6], (HEADS * HD, D), (HEADS * HD) ** -0.5, 0.15625, ((0, 4), (1, 32))),
        "text_len": with_ends(jax.random.randint(key_of[7], (2, PROMPTS), 1, TXT + 1), jax.random.fold_in(key_of[7], 1), 1, TXT).astype(jnp.int32),
        "text_tiles": jax.vmap(lambda own: jax.random.permutation(own, 4))(jax.random.split(key_of[8], 2 * PROMPTS)).reshape((2, PROMPTS, 4)).astype(jnp.int32),
        "step_index": with_ends(jax.random.randint(key_of[9], (PROMPTS,), 0, STEPS), jax.random.fold_in(key_of[9], 1), 0, STEPS - 1).astype(jnp.int32),
    }


GUIDANCE = 4.0
SHIFT_FACTOR = 3.0
EPSILON = 1e-06

def layer_norm(rows):
    mean_value = lax.optimization_barrier(jnp.mean(rows, axis=-1, keepdims=True))
    centred = rows - mean_value
    spread = lax.optimization_barrier(jnp.mean(centred * centred, axis=-1, keepdims=True))
    return centred * lax.rsqrt(spread + EPSILON)

def head_norm(matrix, scaling):
    strength = lax.optimization_barrier(jnp.mean(matrix * matrix, axis=-1, keepdims=True))
    return (matrix * lax.rsqrt(strength + EPSILON) * scaling).astype(jnp.bfloat16)

def sigma_of(position):
    remaining = 1.0 - position / STEPS
    return SHIFT_FACTOR * remaining / (1.0 + (SHIFT_FACTOR - 1.0) * remaining)

def reference(image, text, modulation, w_qkv, q_gain, k_gain, w_proj, text_len, text_tiles, step_index):
    weight_four = w_qkv.reshape(D, HEADS, 3, HD)
    query_weight = weight_four[:, :, 0].reshape(D, HEADS * HD)
    pair_weight = weight_four[:, :, 1:].reshape(D, HEADS * 2 * HD)
    tile_rows = TXT // 4
    offsets = jnp.arange(tile_rows, dtype=jnp.int32)

    def velocity_of(half):

        def one_prompt(prompt):
            image_rows = lax.dynamic_slice_in_dim(image, prompt * IMG, IMG, 0)
            text_rows = lax.dynamic_slice_in_dim(text[half], prompt * TXT, TXT, 0)
            mods = lax.dynamic_index_in_dim(modulation[half], prompt, 0, keepdims=False)
            rows_all = jnp.concatenate([image_rows, text_rows], 0).astype(jnp.float32)
            normed = ((1.0 + mods[1]) * layer_norm(rows_all) + mods[0]).astype(jnp.bfloat16)
            query_sum = jnp.dot(normed[:IMG], query_weight, preferred_element_type=jnp.float32)
            pair_sum = jnp.dot(normed, pair_weight, preferred_element_type=jnp.float32)
            query = head_norm(query_sum.reshape(IMG, HEADS, HD), q_gain)
            pairs = pair_sum.reshape(IMG + TXT, HEADS, 2, HD)
            keys = head_norm(pairs[:, :, 0], k_gain)
            values = pairs[:, :, 1].astype(jnp.bfloat16)
            order_row = lax.dynamic_index_in_dim(text_tiles[half], prompt, 0, keepdims=False)
            length_now = lax.dynamic_index_in_dim(text_len[half], prompt, 0, keepdims=False)
            positions = (order_row[:, None] * tile_rows + offsets[None, :]).reshape(TXT)
            live_keys = jnp.concatenate([jnp.ones((IMG,), bool), positions < length_now])
            scores = jnp.einsum('qhd,khd->hqk', query.astype(jnp.float32), keys.astype(jnp.float32)) * HD ** (-0.5)
            scores = jnp.where(live_keys[None, None, :], scores, -jnp.inf)
            row_max = lax.optimization_barrier(jnp.max(scores, axis=-1, keepdims=True))
            exps = jnp.exp(scores - row_max)
            probs = (exps / lax.optimization_barrier(jnp.sum(exps, axis=-1, keepdims=True))).astype(jnp.bfloat16)
            attended = jnp.einsum('hqk,khd->qhd', probs.astype(jnp.float32), values.astype(jnp.float32))
            attended = attended.astype(jnp.bfloat16).reshape(IMG, HEADS * HD)
            projected = jnp.dot(attended, w_proj, preferred_element_type=jnp.float32)
            return (image_rows.astype(jnp.float32) + mods[2] * projected).astype(jnp.bfloat16)
        return lax.map(one_prompt, jnp.arange(PROMPTS, dtype=jnp.int32)).reshape(IMGTOK, D)
    cond_velocity = velocity_of(0).astype(jnp.float32)
    uncond_velocity = velocity_of(1).astype(jnp.float32)
    guided = uncond_velocity + GUIDANCE * (cond_velocity - uncond_velocity)
    step_now = step_index.astype(jnp.float32)
    step_size = sigma_of(step_now + 1.0) - sigma_of(step_now)
    latent_next = image.astype(jnp.float32) + jnp.repeat(step_size, IMG)[:, None] * guided
    return (guided, latent_next)
```

```python
import functools

import jax
import jax.numpy as jnp
from jax import lax
from jax.experimental import pallas as pl
from jax.experimental.pallas import tpu as pltpu
from jax.sharding import PartitionSpec as P

HD = 128
STEPS = 28
GUIDANCE = 4.0
SHIFT_FACTOR = 3.0
EPSILON = 1e-06
NEG = -1e30


NZ = 8
CS = ("cfg", "seq")


def cs_map(move):
    pairs = []
    for c in range(2):
        for x in range(2):
            for z in range(NZ):
                for k in range(2):
                    c2, x2, z2, k2 = move(c, x, z, k)
                    pairs.append((c * 32 + x * 16 + z * 2 + k, c2 * 32 + x2 * 16 + z2 * 2 + k2))
    return pairs


RING = cs_map(lambda c, x, z, k: (c, x, (z + 1 - 2 * k) % NZ, k))
OTHER_CORE = cs_map(lambda c, x, z, k: (c, x, z, 1 - k))
OTHER_X = cs_map(lambda c, x, z, k: (1 - c, 1 - x, z, k))
OTHER_CFG = cs_map(lambda c, x, z, k: (1 - c, x, z, k))
SPREAD = [
    ((x * 16 + (2 * a + b) * 2 + k) * 4 + t, (x * 16 + (2 * t + b) * 2 + k) * 4 + a)
    for x in range(2)
    for a in range(4)
    for b in range(2)
    for k in range(2)
    for t in range(4)
]


def send(block, route):
    return lax.ppermute(block, CS, route)


def turn(block, shift):
    return lax.ppermute(block, "tp", [(i, (i + shift) % 4) for i in range(4)])


def vmem(n):
    return [pl.BlockSpec(memory_space=pltpu.VMEM)] * n


def call(body, ids, args, outs, scratch=(), flops=0, name=None):
    moved = sum(a.size * a.dtype.itemsize for a in args)
    return pl.pallas_call(
        body,
        out_shape=outs,
        in_specs=[pl.BlockSpec(memory_space=pltpu.SMEM)] + vmem(len(args)),
        out_specs=jax.tree.map(lambda _: pl.BlockSpec(memory_space=pltpu.VMEM), outs),
        scratch_shapes=list(scratch),
        compiler_params=pltpu.CompilerParams(vmem_limit_bytes=40 << 20),
        cost_estimate=pl.CostEstimate(flops=flops, bytes_accessed=moved, transcendentals=0),
        name=name,
    )(ids, *args)


def shape(dims, dtype=jnp.bfloat16):
    return jax.ShapeDtypeStruct(dims, dtype)


def norm_body(ids, own, back, ahead, far_a, far_b, town, tback, tahead, mods, out, pick, raw):
    tp, cfg = ids[3], ids[4]
    rows = out.shape[0]
    imgs = own.shape[0]
    wide = own.shape[1]

    def spot(step):
        return pl.ds(pl.multiple_of(lax.rem(tp + step, 4) * wide, 128), wide)

    raw[0:imgs, spot(0)] = own[...]
    raw[0:imgs, spot(3)] = back[...]
    raw[0:imgs, spot(1)] = ahead[...]
    raw[imgs:rows, spot(0)] = town[...]
    raw[imgs:rows, spot(3)] = tback[...]
    raw[imgs:rows, spot(1)] = tahead[...]
    cut = far_a.shape[0]
    raw[0:cut, spot(2)] = far_a[...]
    raw[cut:rows, spot(2)] = far_b[...]
    width = raw.shape[1]
    block = width // 8
    for side in range(2):
        half = jnp.where(cfg == 0, side, 1 - side)
        at = pl.multiple_of(half * (width // 2) + tp * block, 128)
        pick[side] = raw[0:imgs, pl.ds(at, block)]
    shift = mods[0:1, :]
    scale = 1.0 + mods[1:2, :]

    def step(i, carry):
        here = pl.ds(pl.multiple_of(i * 16, 16), 16)
        x = raw[here, :].astype(jnp.float32)
        mean = jnp.mean(x, axis=-1, keepdims=True)
        x = x - mean
        spread = jnp.mean(x * x, axis=-1, keepdims=True)
        out[here, :] = (scale * (x * lax.rsqrt(spread + EPSILON)) + shift).astype(jnp.bfloat16)
        return carry

    lax.fori_loop(0, rows // 16, step, 0)


def pieces_of(ids, refs):
    core, xh, z = ids[0], ids[1], ids[2]
    way = 1 - 2 * core
    start, r1, r2, r3, r4, e1, e2, e3, e4 = refs
    for ref, dist, mine in (
        (start, 0, True), (r1, -1, True), (r2, -2, True), (r3, -3, True), (r4, -4, True),
        (e1, 1, False), (e2, 2, False), (e3, 3, False), (e4, 4, False),
    ):
        zo = lax.rem(z + way * dist + NZ, NZ)
        for j in range(ref.shape[0]):
            kr, xr = j // 2, j % 2
            flip = kr if mine else 1 - kr
            k = jnp.where(core == 0, flip, 1 - flip)
            x = jnp.where(xh == 0, xr, 1 - xr)
            yield ref, j, x, zo, k


def join_in_body(ids, *refs):
    out = refs[-1]
    for ref, j, x, zo, k in pieces_of(ids, refs[:-1]):
        n = ref.shape[1]
        at = pl.multiple_of((x * 16 + zo * 2 + k) * n, 32)
        out[pl.ds(at, n), :] = ref[j]


def join_out_body(ids, *refs):
    out = refs[-1]
    cfg = ids[4]
    for ref, j, x, zo, k in pieces_of(ids, refs[:-1]):
        n, wide = ref.shape[1], ref.shape[2]
        side = jnp.where(cfg == 0, x, 1 - x)
        at = pl.multiple_of(side * (4 * n) + lax.rem(zo, 2) * (2 * n) + k * n, 32)
        lane = pl.multiple_of((zo // 2) * wide, 128)
        out[pl.ds(at, n), pl.ds(lane, wide)] = ref[j]


def head_norm(m, gain):
    strength = jnp.mean(m * m, axis=-1, keepdims=True)
    return (m * lax.rsqrt(strength + EPSILON) * gain).astype(jnp.bfloat16)


def qkv_body(heads, ids, x, w, q_gain, k_gain, *outs):
    rows = x.shape[0]
    for h in range(heads):
        q_out, kv_out = outs[2 * h], outs[2 * h + 1]
        base = h * 3 * HD
        for r in range(rows // 256):
            here = slice(r * 256, r * 256 + 256)
            xs = x[here, :]
            if (r + 1) * 256 <= q_out.shape[0]:
                q = jnp.dot(xs, w[:, base:base + HD], preferred_element_type=jnp.float32)
                q_out[here, :] = head_norm(q, q_gain[...])
            kv = jnp.dot(xs, w[:, base + HD:base + 3 * HD], preferred_element_type=jnp.float32)
            kv_out[here, 0:HD] = head_norm(kv[:, 0:HD], k_gain[...])
            kv_out[here, HD:2 * HD] = kv[:, HD:].astype(jnp.bfloat16)


NT = (((1,), (1,)), ((), ()))


def attend_body(first, ids, *refs):
    out = refs[-1]
    bias_own, bias_far = refs[-3], refs[-2]
    count = (len(refs) - 3) // 3
    rows = out.shape[0]
    for h in range(count):
        q, own, far = refs[3 * h:3 * h + 3]
        for r in range(rows // 128):
            qs = q[first + r * 128:first + r * 128 + 128, :]
            s1 = lax.dot_general(qs, own[:, 0:HD], NT, preferred_element_type=jnp.float32)
            s2 = lax.dot_general(qs, far[:, 0:HD], NT, preferred_element_type=jnp.float32)
            s1 = s1 * HD ** (-0.5) + bias_own[...]
            s2 = s2 * HD ** (-0.5) + bias_far[...]
            top = jnp.maximum(
                jnp.max(s1, axis=-1, keepdims=True), jnp.max(s2, axis=-1, keepdims=True)
            )
            e1 = jnp.exp(s1 - top)
            e2 = jnp.exp(s2 - top)
            total = jnp.sum(e1, axis=-1, keepdims=True) + jnp.sum(e2, axis=-1, keepdims=True)
            inverse = 1.0 / total
            p1 = (e1 * inverse).astype(jnp.bfloat16)
            p2 = (e2 * inverse).astype(jnp.bfloat16)
            o = jnp.dot(p1, own[:, HD:], preferred_element_type=jnp.float32)
            o = o + jnp.dot(p2, far[:, HD:], preferred_element_type=jnp.float32)
            out[r * 128:r * 128 + 128, h * HD:h * HD + HD] = o.astype(jnp.bfloat16)


def project_body(first, ids, *refs):
    tp = ids[3]
    firsts, rests = refs[0:4], refs[4:8]
    w, pick, gate, keep, away, both = refs[8:]
    rows = keep.shape[0]
    for ref, rest, step in zip(firsts, rests, (0, 3, 1, 2)):
        at = lax.rem(tp + step, 4) * (3 * HD)
        both[:, pl.ds(pl.multiple_of(at, 128), HD)] = ref[first:first + rows, :]
        both[:, pl.ds(pl.multiple_of(at + HD, 128), 2 * HD)] = rest[...]
    half = keep.shape[1]
    for side, out in ((1, away), (0, keep)):
        acc = lax.dot_general(
            both[...], w[side * half:(side + 1) * half, :], NT, preferred_element_type=jnp.float32
        )
        image = pick[side, first:first + rows, :].astype(jnp.float32)
        out[...] = (image + gate[side:side + 1, :] * acc).astype(jnp.bfloat16)


def sigma_of(position):
    remaining = 1.0 - position / STEPS
    return SHIFT_FACTOR * remaining / (1.0 + (SHIFT_FACTOR - 1.0) * remaining)


def ring(start):
    r1 = send(start, RING)
    r2 = send(r1, RING)
    r3 = send(r2, RING)
    r4 = send(r3[:2], RING)
    e1, e2, e3, e4 = (send(r, OTHER_CORE) for r in (r1, r2, r3, r4))
    return [start, r1, r2, r3, r4, e1, e2, e3, e4]


def whole(piece):
    far = send(piece, OTHER_X)
    pair = jnp.stack([piece, far])
    return jnp.concatenate([pair, send(pair, OTHER_CORE)])


def local(image, text, modulation, w_qkv, q_gain, k_gain, w_proj, text_len, text_tiles, step_index):
    cfg = lax.axis_index("cfg")
    seq = lax.axis_index("seq")
    tp = lax.axis_index("tp")
    prompt = seq // 2
    core = seq % 2
    ids = jnp.stack([core, seq // 16, prompt % NZ, tp, cfg]).astype(jnp.int32)
    text = text[0]
    imgs, wide = image.shape
    txts = text.shape[0]
    rows = imgs + txts
    width = 4 * wide

    back, ahead = turn(image, 1), turn(image, -1)
    tback, tahead = turn(text, 1), turn(text, -1)
    cut = rows // 2
    far_a = turn(back[:cut], 1)
    far_b = turn(jnp.concatenate([ahead[cut:], tahead]), -1)

    span = 3 * HD
    pieces = whole(w_qkv)
    set_a = ring(pieces[:, :, :span])
    set_b = ring(pieces[:, :, span:])
    spread = lax.ppermute(w_proj.T, ("seq", "tp"), SPREAD)
    set_c = ring(whole(spread))

    mods = lax.dynamic_index_in_dim(modulation[0], prompt, 0, keepdims=False)
    gates = mods[2].reshape(2, 4, width // 8)
    gates = lax.dynamic_index_in_dim(gates, tp, 1, keepdims=False)
    gates = jnp.where(cfg == 0, gates, gates[::-1])

    length = lax.dynamic_slice(text_len, (cfg, prompt), (1, 1))[0, 0]
    order = lax.dynamic_slice(text_tiles, (cfg, prompt, 0), (1, 1, 4))[0, 0]
    tile = txts // 2

    def bias(side):
        tiles = lax.dynamic_slice_in_dim(order, 2 * side, 2, 0)
        place = (tiles[:, None] * tile + jnp.arange(tile, dtype=jnp.int32)[None, :]).reshape(txts)
        dead = jnp.where(place < length, 0.0, NEG).astype(jnp.float32)
        return jnp.concatenate([jnp.zeros((imgs,), jnp.float32), dead])[None]

    bias_own, bias_far = bias(core), bias(1 - core)

    normed, pick = call(
        norm_body, ids, [image, back, ahead, far_a, far_b, text, tback, tahead, mods],
        [shape((rows, width)), shape((2, imgs, width // 8))],
        [pltpu.VMEM((rows, width), jnp.bfloat16)], name="norm",
    )
    w_a = call(join_in_body, ids, set_a, shape((width, span)), name="join_a")
    w_b = call(join_in_body, ids, set_b, shape((width, 2 * span)), name="join_b")
    w_c = call(join_out_body, ids, set_c, shape((width // 4, 12 * HD)), name="join_c")

    gains = [q_gain[None], k_gain[None]]
    one = [shape((imgs, HD)), shape((rows, 2 * HD))]
    flops = 2 * rows * width * span
    q0, kv0 = call(
        functools.partial(qkv_body, 1), ids, [normed, w_a] + gains, one, flops=flops, name="qkv_a"
    )
    q1, kv1, q2, kv2 = call(
        functools.partial(qkv_body, 2), ids, [normed, w_b] + gains, one + one, flops=2 * flops,
        name="qkv_b",
    )
    far0, far1, far2 = (send(kv, OTHER_CORE) for kv in (kv0, kv1, kv2))
    biases = [bias_own, bias_far]
    work = 4 * imgs * 2 * rows * HD
    att_a = call(
        functools.partial(attend_body, 0), ids, [q0, kv0, far0] + biases,
        shape((imgs, HD)), flops=work, name="attend_a",
    )
    first_all = [att_a] + [turn(att_a, s) for s in (1, -1, 2)]
    half = imgs // 2
    step_now = lax.dynamic_index_in_dim(step_index, prompt, 0, keepdims=False).astype(jnp.float32)
    step_size = sigma_of(step_now + 1.0) - sigma_of(step_now)
    guided, latent = [], []
    for r in range(2):
        att = call(
            functools.partial(attend_body, r * half), ids,
            [q1, kv1, far1, q2, kv2, far2] + biases,
            shape((half, 2 * HD)), flops=work, name=f"attend_b{r}",
        )
        rest_all = [att] + [turn(att, s) for s in (1, -1, 2)]
        keep, away = call(
            functools.partial(project_body, r * half), ids,
            first_all + rest_all + [w_c, pick, gates],
            [shape((half, width // 8))] * 2,
            [pltpu.VMEM((half, 12 * HD), jnp.bfloat16)],
            flops=2 * half * 12 * HD * width // 4, name=f"project{r}",
        )
        keep = keep.astype(jnp.float32)
        other = send(away, OTHER_CFG).astype(jnp.float32)
        cond = jnp.where(cfg == 0, keep, other)
        uncond = jnp.where(cfg == 0, other, keep)
        steer = uncond + GUIDANCE * (cond - uncond)
        own = pick[0, r * half:(r + 1) * half].astype(jnp.float32)
        guided.append(steer)
        latent.append(own + step_size * steer)
    return (jnp.concatenate(guided), jnp.concatenate(latent))


def solution(mesh):
    in_specs = (
        P("seq", "tp"),
        P("cfg", "seq", "tp"),
        P("cfg", None, None, None),
        P("seq", "tp"),
        P(),
        P(),
        P("tp", "seq"),
        P(),
        P(),
        P(),
    )
    out_specs = (P("seq", ("cfg", "tp")), P("seq", ("cfg", "tp")))
    return jax.shard_map(local, mesh=mesh, in_specs=in_specs, out_specs=out_specs, check_vma=False)
```

```python
import functools

import jax
import jax.numpy as jnp
from jax import lax
from jax.experimental import pallas as pl
from jax.experimental.pallas import tpu as pltpu
from jax.sharding import PartitionSpec as P


HD = 128
STEPS = 28
GUIDANCE = 4.0
SHIFT_FACTOR = 3.0
EPSILON = 1e-06
NEG = -1e30


NZ = 8
CS = ("cfg", "seq")


def cs_map(move):
    pairs = []
    for c in range(2):
        for x in range(2):
            for z in range(NZ):
                for k in range(2):
                    c2, x2, z2, k2 = move(c, x, z, k)
                    pairs.append((c * 32 + x * 16 + z * 2 + k, c2 * 32 + x2 * 16 + z2 * 2 + k2))
    return pairs


UP = cs_map(lambda c, x, z, k: (c, x, (z + 1) % NZ, k))
DOWN = cs_map(lambda c, x, z, k: (c, x, (z - 1) % NZ, k))
OTHER_CORE = cs_map(lambda c, x, z, k: (c, x, z, 1 - k))
OTHER_X = cs_map(lambda c, x, z, k: (1 - c, 1 - x, z, k))
OTHER_CFG = cs_map(lambda c, x, z, k: (1 - c, x, z, k))
SPREAD = [
    ((x * 16 + (2 * a + b) * 2 + k) * 4 + t, (x * 16 + (2 * t + b) * 2 + k) * 4 + a)
    for x in range(2)
    for a in range(4)
    for b in range(2)
    for k in range(2)
    for t in range(4)
]


def send(block, route):
    return lax.ppermute(block, CS, route)


def turn(block, shift):
    return lax.ppermute(block, "tp", [(i, (i + shift) % 4) for i in range(4)])


ANY = pl.BlockSpec(memory_space=pl.ANY)
SCALAR = pl.BlockSpec(memory_space=pltpu.SMEM)
LOCAL = pl.BlockSpec(memory_space=pltpu.VMEM)


def call(body, ids, loose, args, outs, scratch=(), flops=0, limit=24, scalars=()):
    moved = sum(a.size * a.dtype.itemsize for a in [*loose, *args])
    return pl.pallas_call(
        body,
        out_shape=outs,
        in_specs=[SCALAR] * (1 + len(scalars)) + [ANY] * len(loose) + [LOCAL] * len(args),
        out_specs=jax.tree.map(lambda _: LOCAL, outs),
        scratch_shapes=list(scratch),
        compiler_params=pltpu.CompilerParams(vmem_limit_bytes=limit << 20),
        cost_estimate=pl.CostEstimate(flops=flops, bytes_accessed=moved, transcendentals=0),
    )(ids, *scalars, *loose, *args)


def shape(dims, dtype=jnp.bfloat16):
    return jax.ShapeDtypeStruct(dims, dtype)


def run(moves, sems):
    copies = [pltpu.make_async_copy(src, dst, sems.at[i]) for i, (src, dst) in enumerate(moves)]
    for copy in copies:
        copy.start()
    return copies


def norm_body(
    ids, lengths, orders, own, near, far, other_near, other_far, town, tback, tahead, tfar, table,
    out, pick, gates, bias, raw, part, part2, stat, mods, sems,
):
    core, tp, cfg, prompt = ids[0], ids[3], ids[4], ids[5]
    rows = out.shape[0]
    imgs, wide = own.shape
    half = imgs // 2
    width = raw.shape[1]
    tiles = width // 128

    def spot(first, size, step):
        lanes = pl.ds(pl.multiple_of(lax.rem(tp + step, 4) * wide, 128), wide)
        return raw.at[pl.ds(first, size), lanes]

    mine = pl.multiple_of(cfg * half, half)
    rest = pl.multiple_of((1 - cfg) * half, half)
    texts = rows - imgs
    copies = run(
        [
            (own, spot(0, imgs, 0)), (town, spot(imgs, texts, 0)),
            (near.at[0], spot(mine, half, 3)), (tback, spot(imgs, texts, 3)),
            (near.at[1], spot(mine, half, 1)), (tahead, spot(imgs, texts, 1)),
            (other_near.at[0], spot(rest, half, 3)), (other_near.at[1], spot(rest, half, 1)),
            (far, spot(mine, half, 2)), (other_far, spot(rest, half, 2)),
            (tfar, spot(imgs, texts, 2)), (table.at[prompt], mods),
        ],
        sems,
    )
    length = lengths[cfg, prompt]
    tile_rows = texts // 2
    lane = lax.broadcasted_iota(jnp.int32, (1, tile_rows), 1)
    for row in range(2):
        part_of = core if row == 0 else 1 - core
        for j in range(2):
            place = orders[cfg, prompt, 2 * part_of + j] * tile_rows + lane
            first = j * tile_rows
            bias[row:row + 1, first:first + tile_rows] = jnp.where(place < length, 0.0, NEG)

    def tile(i, step, j):
        here = pl.ds(pl.multiple_of(i * 32, 32), 32)
        first = lax.rem(tp + step, 4) * wide + j * 128
        return raw[here, pl.ds(pl.multiple_of(first, 128), 128)].astype(jnp.float32)

    def rows_at(i):
        return pl.ds(pl.multiple_of(i * 32, 32), 32)

    copies[0].wait()
    copies[1].wait()

    def base(i, carry):
        mid = jnp.mean(tile(i, 0, 0), axis=-1, keepdims=True)
        stat[rows_at(i), :] = jnp.broadcast_to(mid, (32, 128))
        return carry

    def gather(steps, i, first, second):
        mid = stat[rows_at(i), :]
        for step in steps:
            for j in range(wide // 128):
                d = tile(i, step, j) - mid
                first = first + d
                second = second + d * d
        part[rows_at(i), :] = first
        part2[rows_at(i), :] = second

    def open_sums(i, carry):
        zero = jnp.zeros((32, 128), jnp.float32)
        gather((0,), i, zero, zero)
        return carry

    def close_sums(i, carry):
        gather((1, 2, 3), i, part[rows_at(i), :], part2[rows_at(i), :])
        return carry

    lax.fori_loop(0, rows // 32, base, 0, unroll=2)
    lax.fori_loop(0, rows // 32, open_sums, 0)
    for copy in copies[2:]:
        copy.wait()
    block = width // 8
    moves = []
    for side in range(2):
        part_of = jnp.where(cfg == 0, side, 1 - side)
        at = pl.multiple_of(part_of * (width // 2) + tp * block, 128)
        moves.append((raw.at[0:imgs, pl.ds(at, block)], pick.at[side]))
        gates[side:side + 1, :] = mods[2:3, pl.ds(at, block)]
    picks = run(moves, sems)

    lax.fori_loop(0, rows // 32, close_sums, 0)
    shift_mean = jnp.sum(part[...], axis=-1, keepdims=True) * (1.0 / width)
    spread = jnp.sum(part2[...], axis=-1, keepdims=True) * (1.0 / width)
    spread = jnp.maximum(spread - shift_mean * shift_mean, 0.0)
    stat[...] = stat[...] + shift_mean
    part[...] = jnp.broadcast_to(lax.rsqrt(spread + EPSILON), part.shape)

    def finish(i, carry):
        here = pl.ds(pl.multiple_of(i * 32, 32), 32)
        mid, rate = stat[here, :], part[here, :]
        for j in range(tiles):
            lanes = slice(j * 128, (j + 1) * 128)
            scale = 1.0 + mods[1:2, lanes]
            x = raw[here, lanes].astype(jnp.float32)
            y = scale * ((x - mid) * rate) + mods[0:1, lanes]
            out[here, lanes] = y.astype(jnp.bfloat16)
        return carry

    lax.fori_loop(0, rows // 32, finish, 0)
    for copy in picks:
        copy.wait()


def prep_body(ids, image, w_qkv, mine, own_w, sems):
    half = mine.shape[0]
    moves = [(image.at[pl.ds(pl.multiple_of(ids[4] * half, half), half), :], mine)]
    copies = run(moves, sems)
    at = 0
    for i, j in ((0, 1), (3, 4), (6, 7), (1, 3), (4, 6), (7, 9)):
        n = (j - i) * HD
        own_w[:, at:at + n] = w_qkv[:, i * HD:j * HD]
        at += n
    for copy in copies:
        copy.wait()


def spots(ids, groups):
    core, xh, z = ids[0], ids[1], ids[2]
    for src, dist, flip, xr in groups:
        zo = lax.rem(z + dist + NZ, NZ)
        k = jnp.where(core == 0, flip, 1 - flip)
        x = jnp.where(xh == 0, xr, 1 - xr)
        yield src, x, zo, k


def ring_groups(refs):
    own, f0, e0, last, f4, e4 = refs[:6]
    yield own, 0, 0, 0
    yield f0, 0, 0, 1
    yield e0.at[0], 0, 1, 0
    yield e0.at[1], 0, 1, 1
    yield last, -4, 0, 0
    yield f4, -4, 0, 1
    yield e4.at[0], -4, 1, 0
    yield e4.at[1], -4, 1, 1
    for i, ref in enumerate(refs[6:]):
        dist = 1 + i // 4
        flip, xr = (i % 4) // 2, i % 2
        yield ref.at[0], -dist, flip, xr
        yield ref.at[1], dist, flip, xr


PARTS = 18


def pull_in(ids, refs, pieces, sems):
    moves = []
    for src, x, zo, k in spots(ids, ring_groups(refs)):
        n = src.shape[0]
        at = pl.ds(pl.multiple_of((x * 16 + zo * 2 + k) * n, 32), n)
        for lanes, w in pieces:
            moves.append((src.at[:, lanes], w.at[at, :]))
    return run(moves, sems)


def join_out_body(ids, near, far, swap, out, sems):
    cfg = ids[4]
    groups = []
    for j, dist in enumerate((0, -1, 1, -2, 2, -3, 3, -4)):
        groups += [(near.at[j], dist, 0, 0), (far.at[j], dist, 0, 1)]
        groups += [(swap.at[0, j], dist, 1, 0), (swap.at[1, j], dist, 1, 1)]
    moves = []
    for src, x, zo, k in spots(ids, groups):
        n, wide = src.shape
        side = jnp.where(cfg == 0, x, 1 - x)
        at = pl.multiple_of(side * (4 * n) + lax.rem(zo, 2) * (2 * n) + k * n, 32)
        lane = pl.multiple_of((zo // 2) * wide, 128)
        moves.append((src, out.at[pl.ds(at, n), pl.ds(lane, wide)]))
    for copy in run(moves, sems):
        copy.wait()


def head_norm(m, gain):
    strength = jnp.mean(m * m, axis=-1, keepdims=True)
    return (m * lax.rsqrt(strength + EPSILON) * gain).astype(jnp.bfloat16)


def pairs_body(ids, *refs):
    parts, (x, gain, out, w_q, w, sems) = refs[:PARTS], refs[PARTS:]
    rows, span = out.shape
    lanes_q, lanes_w = slice(0, span // 2), slice(span // 2, span // 2 + span)
    copies = pull_in(ids, parts, [(lanes_w, w), (lanes_q, w_q)], sems)
    for copy in copies[::2]:
        copy.wait()

    def step(h, carry):
        lanes = pl.ds(pl.multiple_of(h * 2 * HD, 2 * HD), 2 * HD)
        first = pl.ds(pl.multiple_of(h * 2 * HD, HD), HD)
        second = pl.ds(pl.multiple_of(h * 2 * HD + HD, HD), HD)
        for r in range(rows // 256):
            here = slice(r * 256, r * 256 + 256)
            kv = jnp.dot(x[here, :], w[:, lanes], preferred_element_type=jnp.float32)
            out[here, first] = head_norm(kv[:, 0:HD], gain[...])
            out[here, second] = kv[:, HD:].astype(jnp.bfloat16)
        return carry

    lax.fori_loop(0, span // (2 * HD), step, 0)
    for copy in copies[1::2]:
        copy.wait()


def queries_body(ids, x, w, gain, out):
    imgs, span = out.shape
    for r in range(imgs // 256):
        here = slice(r * 256, r * 256 + 256)
        q = jnp.dot(x[here, :], w[...], preferred_element_type=jnp.float32)
        for h in range(span // HD):
            lanes = slice(h * HD, (h + 1) * HD)
            out[here, lanes] = head_norm(q[:, lanes], gain[...])


NT = (((1,), (1,)), ((), ()))


SOFT = HD ** (-0.5) * 1.4426950408889634


def attend_body(first, ids, q, own, far, bias, out):
    rows, span = out.shape
    tiles = rows // 128
    texts = bias.shape[1]
    imgs = own.shape[0] - texts

    def step(i, carry):
        h, r = i // tiles, lax.rem(i, tiles)
        head = pl.ds(pl.multiple_of(h * HD, HD), HD)
        key = pl.ds(pl.multiple_of(h * 2 * HD, HD), HD)
        value = pl.ds(pl.multiple_of(h * 2 * HD + HD, HD), HD)
        qs = q[pl.ds(pl.multiple_of(first + r * 128, 128), 128), head]
        scores, spans = [], []
        for side, ref in enumerate((own, far)):
            for here in (slice(0, imgs), slice(imgs, imgs + texts)):
                s = lax.dot_general(qs, ref[here, key], NT, preferred_element_type=jnp.float32)
                s = s * SOFT
                if here.start:
                    s = s + bias[side:side + 1, :]
                scores.append(s)
                spans.append((ref, here))
        top = functools.reduce(
            jnp.maximum, [jnp.max(s, axis=-1, keepdims=True) for s in scores]
        )
        powers = [jnp.exp2(s - top) for s in scores]
        total = functools.reduce(
            jnp.add, [jnp.sum(e, axis=-1, keepdims=True) for e in powers]
        )
        inverse = 1.0 / total
        o = jnp.zeros((128, HD), jnp.float32)
        for e, (ref, here) in zip(powers, spans):
            p = (e * inverse).astype(jnp.bfloat16)
            o = o + jnp.dot(p, ref[here, value], preferred_element_type=jnp.float32)
        out[pl.ds(pl.multiple_of(r * 128, 128), 128), head] = o.astype(jnp.bfloat16)
        return carry

    lax.fori_loop(0, span // HD * tiles, step, 0, unroll=2)


def project_body(first, ids, *refs):
    tp = ids[3]
    w, pick, gate, keep, away, both = refs[4:]
    rows = keep.shape[0]
    for ref, step in zip(refs[:4], (0, 3, 1, 2)):
        at = lax.rem(tp + step, 4) * (3 * HD)
        both[:, pl.ds(pl.multiple_of(at, 128), 3 * HD)] = ref[...]
    half = keep.shape[1]
    for side, out in ((1, away), (0, keep)):
        acc = lax.dot_general(
            both[...], w[side * half:(side + 1) * half, :], NT, preferred_element_type=jnp.float32
        )
        image = pick[side, first:first + rows, :].astype(jnp.float32)
        out[...] = (image + gate[side:side + 1, :] * acc).astype(jnp.bfloat16)


def sigma_of(position):
    remaining = 1.0 - position / STEPS
    return SHIFT_FACTOR * remaining / (1.0 + (SHIFT_FACTOR - 1.0) * remaining)


def final_body(ids, steps, *refs):
    keeps, others, (pick, guided, latent) = refs[0:2], refs[2:4], refs[4:]
    cfg, prompt = ids[4], ids[5]
    half, block = keeps[0].shape
    now = jnp.full((1, block), steps[prompt], jnp.int32).astype(jnp.float32)
    step_size = sigma_of(now + 1.0) - sigma_of(now)
    for r in range(2):
        here = slice(r * half, (r + 1) * half)
        keep = keeps[r][...].astype(jnp.float32)
        other = others[r][...].astype(jnp.float32)
        cond = jnp.where(cfg == 0, keep, other)
        uncond = jnp.where(cfg == 0, other, keep)
        steer = uncond + GUIDANCE * (cond - uncond)
        guided[here, :] = steer
        latent[here, :] = pick[0, here, :].astype(jnp.float32) + step_size * steer


def inner(image, text, modulation, w_qkv, q_gain, k_gain, w_proj, text_len, text_tiles, step_index):
    cfg = lax.axis_index("cfg")
    seq = lax.axis_index("seq")
    tp = lax.axis_index("tp")
    prompt = seq // 2
    core = seq % 2
    at = lax.iota(jnp.int32, 8)
    ids = jnp.where(at == 0, core, jnp.where(at == 1, seq // 16, cfg))
    ids = jnp.where(at == 2, prompt % NZ, jnp.where(at == 3, tp, ids))
    ids = jnp.where(at == 5, prompt, ids).astype(jnp.int32)
    ids, image, w_qkv, w_proj = lax.optimization_barrier((ids, image, w_qkv, w_proj))
    text = text[0]
    imgs, wide = image.shape
    txts = text.shape[0]
    rows = imgs + txts
    width = 4 * wide

    half = imgs // 2
    mine, own_w = call(
        prep_body, ids, [image], [w_qkv],
        [shape((half, wide)), shape(w_qkv.shape)],
        [pltpu.SemaphoreType.DMA((1,))], limit=6,
    )
    far, back, ahead = (turn(mine, s) for s in (2, 1, -1))
    tback, tahead, tfar = (turn(text, s) for s in (1, -1, 2))
    near = jnp.stack([back, ahead])
    other_near = send(near, OTHER_CFG)
    other_far = send(far, OTHER_CFG)

    span = 3 * HD
    last = 3 * span
    spread = lax.ppermute(w_proj.T, ("seq", "tp"), SPREAD)
    own_all = jnp.concatenate([own_w, spread], -1)
    f0 = send(own_w, OTHER_X)
    e0 = send(jnp.stack([own_w, f0]), OTHER_CORE)
    up, down = own_all, own_all
    ring, tails = [], [own_all]
    for _ in range(1, 4):
        up, down = send(up, UP), send(down, DOWN)
        tails += [up, down]
        here = jnp.stack([up[:, :last], down[:, :last]])
        there = send(here, OTHER_X)
        ring += [here, there, send(here, OTHER_CORE), send(there, OTHER_CORE)]
    up = send(up, UP)
    tails.append(up)
    end = up[:, :last]
    f4 = send(end, OTHER_X)
    e4 = send(jnp.stack([end, f4]), OTHER_CORE)
    every = [own_w, f0, e0, end, f4, e4] + ring
    near_c = jnp.stack([t[:, last:] for t in tails])
    away_c = send(near_c, OTHER_X)
    swap_c = send(jnp.stack([near_c, away_c]), OTHER_CORE)

    normed, pick, gates, bias = call(
        norm_body, ids,
        [image, near, far, other_near, other_far, text, tback, tahead, tfar, modulation[0]], [],
        [
            shape((rows, width)), shape((2, imgs, width // 8)),
            shape((2, width // 8), jnp.float32), shape((2, txts), jnp.float32),
        ],
        [
            pltpu.VMEM((rows, width), jnp.bfloat16),
            pltpu.VMEM((rows, 128), jnp.float32),
            pltpu.VMEM((rows, 128), jnp.float32),
            pltpu.VMEM((rows, 128), jnp.float32),
            pltpu.VMEM((3, width), jnp.float32),
            pltpu.SemaphoreType.DMA((12,)),
        ],
        limit=16, scalars=[text_len, text_tiles],
    )
    sems = pltpu.SemaphoreType.DMA((32,))
    flops = 2 * width * 3 * HD
    kv, w_q = call(
        pairs_body, ids, every, [normed, k_gain[None]],
        [shape((rows, 2 * span)), shape((width, span))],
        [pltpu.VMEM((width, 2 * span), jnp.bfloat16), pltpu.SemaphoreType.DMA((64,))],
        flops=2 * rows * flops, limit=16,
    )
    kv_far = send(kv, OTHER_CORE)
    q = call(
        queries_body, ids, [], [normed, w_q, q_gain[None]], shape((imgs, span)),
        flops=imgs * flops, limit=12,
    )
    w_c = call(
        join_out_body, ids, [near_c, away_c, swap_c], [], shape((width // 4, 12 * HD)),
        [sems], limit=6,
    )
    work = 4 * half * 6 * rows * HD
    keeps, others = [], []
    for r in range(2):
        att = call(
            functools.partial(attend_body, r * half), ids, [],
            [q, kv, kv_far, bias], shape((half, span)), flops=work,
            limit=10,
        )
        all_att = [att] + [turn(att, s) for s in (1, -1, 2)]
        keep, away = call(
            functools.partial(project_body, r * half), ids, [], all_att + [w_c, pick, gates],
            [shape((half, width // 8))] * 2,
            [pltpu.VMEM((half, 12 * HD), jnp.bfloat16)],
            flops=2 * half * 12 * HD * width // 4, limit=10,
        )
        keeps.append(keep)
        others.append(send(away, OTHER_CFG))
    out = shape((imgs, width // 8), jnp.float32)
    return call(
        final_body, ids, [], keeps + others + [pick], [out, out], scalars=[step_index],
        limit=10,
    )


def solution(mesh):
    in_specs = (
        P("seq", "tp"),
        P("cfg", "seq", "tp"),
        P("cfg", None, None, None),
        P("seq", "tp"),
        P(),
        P(),
        P("tp", "seq"),
        P(),
        P(),
        P(),
    )
    out_specs = (P("seq", ("cfg", "tp")), P("seq", ("cfg", "tp")))
    return jax.shard_map(inner, mesh=mesh, in_specs=in_specs, out_specs=out_specs, check_vma=False)
```

```python
import functools

import jax
import jax.numpy as jnp
from jax import lax
from jax.experimental import pallas as pl
from jax.experimental.pallas import tpu as pltpu
from jax.sharding import PartitionSpec as P


HD = 128
STEPS = 28
GUIDANCE = 4.0
SHIFT_FACTOR = 3.0
EPSILON = 1e-06
NEG = -1e30


NZ = 8
CS = ("cfg", "seq")


def cs_map(move):
    pairs = []
    for c in range(2):
        for x in range(2):
            for z in range(NZ):
                for k in range(2):
                    c2, x2, z2, k2 = move(c, x, z, k)
                    pairs.append((c * 32 + x * 16 + z * 2 + k, c2 * 32 + x2 * 16 + z2 * 2 + k2))
    return pairs


UP = cs_map(lambda c, x, z, k: (c, x, (z + 1) % NZ, k))
DOWN = cs_map(lambda c, x, z, k: (c, x, (z - 1) % NZ, k))
OTHER_CORE = cs_map(lambda c, x, z, k: (c, x, z, 1 - k))
OTHER_X = cs_map(lambda c, x, z, k: (1 - c, 1 - x, z, k))
OTHER_CFG = cs_map(lambda c, x, z, k: (1 - c, x, z, k))
LANDS = {0: (-3, 4), 1: (2, 3), 2: (0, 1), 3: (-2, -1)}
SPREAD = [
    (
        (x * 16 + (2 * a + b) * 2 + k) * 4 + (a + d) % 4,
        (x * 16 + (2 * a + LANDS[d][b]) % NZ * 2 + k) * 4 + a,
    )
    for x in range(2)
    for a in range(4)
    for b in range(2)
    for k in range(2)
    for d in range(4)
]


def send(block, route):
    return lax.ppermute(block, CS, route)


def turn(block, shift):
    return lax.ppermute(block, "tp", [(i, (i + shift) % 4) for i in range(4)])


ANY = pl.BlockSpec(memory_space=pl.ANY)
SCALAR = pl.BlockSpec(memory_space=pltpu.SMEM)
LOCAL = pl.BlockSpec(memory_space=pltpu.VMEM)


def call(body, ids, loose, args, outs, scratch=(), flops=0, limit=24, scalars=()):
    moved = sum(a.size * a.dtype.itemsize for a in [*loose, *args])
    return pl.pallas_call(
        body,
        out_shape=outs,
        in_specs=[SCALAR] * (1 + len(scalars)) + [ANY] * len(loose) + [LOCAL] * len(args),
        out_specs=jax.tree.map(lambda _: LOCAL, outs),
        scratch_shapes=list(scratch),
        compiler_params=pltpu.CompilerParams(vmem_limit_bytes=limit << 20),
        cost_estimate=pl.CostEstimate(flops=flops, bytes_accessed=moved, transcendentals=0),
    )(ids, *scalars, *loose, *args)


def shape(dims, dtype=jnp.bfloat16):
    return jax.ShapeDtypeStruct(dims, dtype)


def run(moves, sems):
    copies = [pltpu.make_async_copy(src, dst, sems.at[i]) for i, (src, dst) in enumerate(moves)]
    for copy in copies:
        copy.start()
    return copies


def norm_body(
    ids, lengths, orders, own, near, far, other_near, other_far, town, tback, tahead, tfar, table,
    out, pick, gates, bias, raw, part, part2, stat, mods, sems,
):
    core, tp, cfg, prompt = ids[0], ids[3], ids[4], ids[5]
    rows = out.shape[0]
    imgs, wide = own.shape
    half = imgs // 2
    width = raw.shape[1]
    tiles = width // 128

    def spot(first, size, step):
        lanes = pl.ds(pl.multiple_of(lax.rem(tp + step, 4) * wide, 128), wide)
        return raw.at[pl.ds(first, size), lanes]

    mine = pl.multiple_of(cfg * half, half)
    rest = pl.multiple_of((1 - cfg) * half, half)
    texts = rows - imgs
    copies = run(
        [
            (own, spot(0, imgs, 0)), (town, spot(imgs, texts, 0)),
            (near.at[0], spot(mine, half, 3)), (tback, spot(imgs, texts, 3)),
            (near.at[1], spot(mine, half, 1)), (tahead, spot(imgs, texts, 1)),
            (other_near.at[0], spot(rest, half, 3)), (other_near.at[1], spot(rest, half, 1)),
            (far, spot(mine, half, 2)), (other_far, spot(rest, half, 2)),
            (tfar, spot(imgs, texts, 2)), (table.at[prompt], mods),
        ],
        sems,
    )
    length = lengths[cfg, prompt]
    tile_rows = texts // 2
    lane = lax.broadcasted_iota(jnp.int32, (1, tile_rows), 1)
    for row in range(2):
        part_of = core if row == 0 else 1 - core
        for j in range(2):
            place = orders[cfg, prompt, 2 * part_of + j] * tile_rows + lane
            first = j * tile_rows
            bias[row:row + 1, first:first + tile_rows] = jnp.where(place < length, 0.0, NEG)

    def tile(i, step, j):
        here = pl.ds(pl.multiple_of(i * 32, 32), 32)
        first = lax.rem(tp + step, 4) * wide + j * 128
        return raw[here, pl.ds(pl.multiple_of(first, 128), 128)].astype(jnp.float32)

    def rows_at(i):
        return pl.ds(pl.multiple_of(i * 32, 32), 32)

    copies[0].wait()
    copies[1].wait()

    def base(i, carry):
        mid = jnp.mean(tile(i, 0, 0), axis=-1, keepdims=True)
        stat[rows_at(i), :] = jnp.broadcast_to(mid, (32, 128))
        return carry

    def gather(steps, i, first, second):
        mid = stat[rows_at(i), :]
        for step in steps:
            for j in range(wide // 128):
                d = tile(i, step, j) - mid
                first = first + d
                second = second + d * d
        part[rows_at(i), :] = first
        part2[rows_at(i), :] = second

    def open_sums(i, carry):
        zero = jnp.zeros((32, 128), jnp.float32)
        gather((0,), i, zero, zero)
        return carry

    def close_sums(i, carry):
        gather((1, 2, 3), i, part[rows_at(i), :], part2[rows_at(i), :])
        return carry

    lax.fori_loop(0, rows // 32, base, 0, unroll=2)
    lax.fori_loop(0, rows // 32, open_sums, 0)
    for copy in copies[2:]:
        copy.wait()
    block = width // 8
    moves = []
    for side in range(2):
        part_of = jnp.where(cfg == 0, side, 1 - side)
        at = pl.multiple_of(part_of * (width // 2) + tp * block, 128)
        moves.append((raw.at[0:imgs, pl.ds(at, block)], pick.at[side]))
        gates[side:side + 1, :] = mods[2:3, pl.ds(at, block)]
    picks = run(moves, sems)

    lax.fori_loop(0, rows // 32, close_sums, 0)
    shift_mean = jnp.sum(part[...], axis=-1, keepdims=True) * (1.0 / width)
    spread = jnp.sum(part2[...], axis=-1, keepdims=True) * (1.0 / width)
    spread = jnp.maximum(spread - shift_mean * shift_mean, 0.0)
    stat[...] = stat[...] + shift_mean
    part[...] = jnp.broadcast_to(lax.rsqrt(spread + EPSILON), part.shape)

    def finish(i, carry):
        here = pl.ds(pl.multiple_of(i * 32, 32), 32)
        mid, rate = stat[here, :], part[here, :]
        for j in range(tiles):
            lanes = slice(j * 128, (j + 1) * 128)
            scale = 1.0 + mods[1:2, lanes]
            x = raw[here, lanes].astype(jnp.float32)
            y = scale * ((x - mid) * rate) + mods[0:1, lanes]
            out[here, lanes] = y.astype(jnp.bfloat16)
        return carry

    lax.fori_loop(0, rows // 32, finish, 0)
    for copy in picks:
        copy.wait()


def prep_body(ids, image, w_qkv, mine, own_w, sems):
    half = mine.shape[0]
    moves = [(image.at[pl.ds(pl.multiple_of(ids[4] * half, half), half), :], mine)]
    copies = run(moves, sems)
    at = 0
    for i, j in ((0, 1), (3, 4), (6, 7), (1, 3), (4, 6), (7, 9)):
        n = (j - i) * HD
        own_w[:, at:at + n] = w_qkv[:, i * HD:j * HD]
        at += n
    for copy in copies:
        copy.wait()


def spots(ids, groups):
    core, xh, z = ids[0], ids[1], ids[2]
    for src, dist, flip, xr in groups:
        zo = lax.rem(z + dist + NZ, NZ)
        k = jnp.where(core == 0, flip, 1 - flip)
        x = jnp.where(xh == 0, xr, 1 - xr)
        yield src, x, zo, k


def ring_groups(refs):
    own, f0, e0, last, f4, e4 = refs[:6]
    yield own, 0, 0, 0
    yield f0, 0, 0, 1
    yield e0.at[0], 0, 1, 0
    yield e0.at[1], 0, 1, 1
    yield last, -4, 0, 0
    yield f4, -4, 0, 1
    yield e4.at[0], -4, 1, 0
    yield e4.at[1], -4, 1, 1
    for i, ref in enumerate(refs[6:]):
        dist, flip = 1 + i // 2, i % 2
        for xr in range(2):
            yield ref.at[xr, 0], -dist, flip, xr
            yield ref.at[xr, 1], dist, flip, xr


PARTS = 12


def pull_in(ids, refs, pieces, sems):
    moves = []
    for src, x, zo, k in spots(ids, ring_groups(refs)):
        n = src.shape[0]
        at = pl.ds(pl.multiple_of((x * 16 + zo * 2 + k) * n, 32), n)
        for lanes, w in pieces:
            moves.append((src.at[:, lanes], w.at[at, :]))
    return run(moves, sems)


def join_out_body(ids, near, far, swap, out, sems):
    tp, cfg = ids[3], ids[4]
    groups = []
    for j, dist in enumerate((0, -1, 1, -2, 2, -3, 3, -4)):
        groups += [(near.at[j], dist, 0, 0), (far.at[j], dist, 0, 1)]
        groups += [(swap.at[0, j], dist, 1, 0), (swap.at[1, j], dist, 1, 1)]
    moves = []
    for src, x, zo, k in spots(ids, groups):
        n, wide = src.shape
        side = jnp.where(cfg == 0, x, 1 - x)
        place = lax.rem(zo - 2 * tp + NZ, NZ)
        pair, odd = place // 2, lax.rem(place, 2)
        b = jnp.where(pair == 2, 1 - odd, odd)
        at = pl.multiple_of(side * (4 * n) + b * (2 * n) + k * n, 32)
        lane = pl.multiple_of(lax.rem(tp + 6 - pair, 4) * wide, 128)
        moves.append((src, out.at[pl.ds(at, n), pl.ds(lane, wide)]))
    for copy in run(moves, sems):
        copy.wait()


def head_norm(m, gain):
    strength = jnp.mean(m * m, axis=-1, keepdims=True)
    return (m * lax.rsqrt(strength + EPSILON) * gain).astype(jnp.bfloat16)


def pairs_body(ids, *refs):
    parts, (x, gain, out, w_q, w, sems) = refs[:PARTS], refs[PARTS:]
    rows, span = out.shape
    lanes_q, lanes_w = slice(0, span // 2), slice(span // 2, span // 2 + span)
    copies = pull_in(ids, parts, [(lanes_w, w), (lanes_q, w_q)], sems)
    for copy in copies[::2]:
        copy.wait()

    def step(h, carry):
        lanes = pl.ds(pl.multiple_of(h * 2 * HD, 2 * HD), 2 * HD)
        first = pl.ds(pl.multiple_of(h * 2 * HD, HD), HD)
        second = pl.ds(pl.multiple_of(h * 2 * HD + HD, HD), HD)
        for r in range(rows // 256):
            here = slice(r * 256, r * 256 + 256)
            kv = jnp.dot(x[here, :], w[:, lanes], preferred_element_type=jnp.float32)
            out[here, first] = head_norm(kv[:, 0:HD], gain[...])
            out[here, second] = kv[:, HD:].astype(jnp.bfloat16)
        return carry

    lax.fori_loop(0, span // (2 * HD), step, 0)
    for copy in copies[1::2]:
        copy.wait()


def queries_body(ids, x, w, gain, out):
    imgs, span = out.shape

    def step(r, carry):
        here = pl.ds(pl.multiple_of(r * 256, 256), 256)
        q = jnp.dot(x[here, :], w[...], preferred_element_type=jnp.float32)
        for h in range(span // HD):
            lanes = slice(h * HD, (h + 1) * HD)
            out[here, lanes] = head_norm(q[:, lanes], gain[...])
        return carry

    lax.fori_loop(0, imgs // 256, step, 0)


NT = (((1,), (1,)), ((), ()))


SOFT = HD ** (-0.5) * 1.4426950408889634


def attend_body(first, ids, q, own, far, bias, out):
    rows, span = out.shape
    tiles = rows // 128
    texts = bias.shape[1]
    imgs = own.shape[0] - texts

    def step(i, carry):
        h, r = i // tiles, lax.rem(i, tiles)
        head = pl.ds(pl.multiple_of(h * HD, HD), HD)
        key = pl.ds(pl.multiple_of(h * 2 * HD, HD), HD)
        value = pl.ds(pl.multiple_of(h * 2 * HD + HD, HD), HD)
        qs = q[pl.ds(pl.multiple_of(first + r * 128, 128), 128), head]
        scores, spans = [], []
        for side, ref in enumerate((own, far)):
            for here in (slice(0, imgs), slice(imgs, imgs + texts)):
                s = lax.dot_general(qs, ref[here, key], NT, preferred_element_type=jnp.float32)
                s = s * SOFT
                if here.start:
                    s = s + bias[side:side + 1, :]
                scores.append(s)
                spans.append((ref, here))
        top = functools.reduce(
            jnp.maximum, [jnp.max(s, axis=-1, keepdims=True) for s in scores]
        )
        powers = [jnp.exp2(s - top) for s in scores]
        total = functools.reduce(
            jnp.add, [jnp.sum(e, axis=-1, keepdims=True) for e in powers]
        )
        inverse = 1.0 / total
        o = jnp.zeros((128, HD), jnp.float32)
        for e, (ref, here) in zip(powers, spans):
            p = (e * inverse).astype(jnp.bfloat16)
            o = o + jnp.dot(p, ref[here, value], preferred_element_type=jnp.float32)
        out[pl.ds(pl.multiple_of(r * 128, 128), 128), head] = o.astype(jnp.bfloat16)
        return carry

    lax.fori_loop(0, span // HD * tiles, step, 0, unroll=2)


def project_body(first, ids, *refs):
    tp = ids[3]
    w, pick, gate, keep, away, both = refs[4:]
    rows = keep.shape[0]
    for ref, step in zip(refs[:4], (0, 3, 1, 2)):
        at = lax.rem(tp + step, 4) * (3 * HD)
        both[:, pl.ds(pl.multiple_of(at, 128), 3 * HD)] = ref[...]
    half = keep.shape[1]
    for side, out in ((1, away), (0, keep)):
        acc = lax.dot_general(
            both[...], w[side * half:(side + 1) * half, :], NT, preferred_element_type=jnp.float32
        )
        image = pick[side, first:first + rows, :].astype(jnp.float32)
        out[...] = (image + gate[side:side + 1, :] * acc).astype(jnp.bfloat16)


def sigma_of(position):
    remaining = 1.0 - position / STEPS
    return SHIFT_FACTOR * remaining / (1.0 + (SHIFT_FACTOR - 1.0) * remaining)


def final_body(ids, steps, *refs):
    keeps, others, (pick, guided, latent) = refs[0:2], refs[2:4], refs[4:]
    cfg, prompt = ids[4], ids[5]
    half, block = keeps[0].shape
    now = jnp.full((1, block), steps[prompt], jnp.int32).astype(jnp.float32)
    step_size = sigma_of(now + 1.0) - sigma_of(now)
    for r in range(2):
        here = slice(r * half, (r + 1) * half)
        keep = keeps[r][...].astype(jnp.float32)
        other = others[r][...].astype(jnp.float32)
        cond = jnp.where(cfg == 0, keep, other)
        uncond = jnp.where(cfg == 0, other, keep)
        steer = uncond + GUIDANCE * (cond - uncond)
        guided[here, :] = steer
        latent[here, :] = pick[0, here, :].astype(jnp.float32) + step_size * steer


def inner(image, text, modulation, w_qkv, q_gain, k_gain, w_proj, text_len, text_tiles, step_index):
    cfg = lax.axis_index("cfg")
    seq = lax.axis_index("seq")
    tp = lax.axis_index("tp")
    prompt = seq // 2
    core = seq % 2
    at = lax.iota(jnp.int32, 8)
    ids = jnp.where(at == 0, core, jnp.where(at == 1, seq // 16, cfg))
    ids = jnp.where(at == 2, prompt % NZ, jnp.where(at == 3, tp, ids))
    ids = jnp.where(at == 5, prompt, ids).astype(jnp.int32)
    ids, image, w_qkv, w_proj = lax.optimization_barrier((ids, image, w_qkv, w_proj))
    text = text[0]
    imgs, wide = image.shape
    txts = text.shape[0]
    rows = imgs + txts
    width = 4 * wide

    half = imgs // 2
    mine, own_w = call(
        prep_body, ids, [image], [w_qkv],
        [shape((half, wide)), shape(w_qkv.shape)],
        [pltpu.SemaphoreType.DMA((1,))], limit=6,
    )
    far, back, ahead = (turn(mine, s) for s in (2, 1, -1))
    tback, tahead, tfar = (turn(text, s) for s in (1, -1, 2))
    near = jnp.stack([back, ahead])
    other_near = send(near, OTHER_CFG)
    other_far = send(far, OTHER_CFG)

    span = 3 * HD
    last = 3 * span
    spread = lax.ppermute(w_proj.T, ("seq", "tp"), SPREAD)
    f0 = send(own_w, OTHER_X)
    e0 = send(jnp.stack([own_w, f0]), OTHER_CORE)
    up = down = own_all = jnp.concatenate([own_w, spread], -1)
    ring, tails = [], [own_all[:, last:]]
    for _ in range(1, 4):
        up, down = send(up, UP), send(down, DOWN)
        tails += [up[:, last:], down[:, last:]]
        here = jnp.stack([up[:, :last], down[:, :last]])
        there = send(here, OTHER_X)
        pair = jnp.stack([here, there])
        ring += [pair, send(pair, OTHER_CORE)]
    up = send(up, UP)
    tails.append(up[:, last:])
    end = up[:, :last]
    f4 = send(end, OTHER_X)
    e4 = send(jnp.stack([end, f4]), OTHER_CORE)
    every = [own_w, f0, e0, end, f4, e4] + ring
    near_c = jnp.stack(tails)
    away_c = send(near_c, OTHER_X)
    both_c = jnp.stack([near_c, away_c])
    swap_c = send(both_c, OTHER_CORE)

    normed, pick, gates, bias = call(
        norm_body, ids,
        [image, near, far, other_near, other_far, text, tback, tahead, tfar, modulation[0]], [],
        [
            shape((rows, width)), shape((2, imgs, width // 8)),
            shape((2, width // 8), jnp.float32), shape((2, txts), jnp.float32),
        ],
        [
            pltpu.VMEM((rows, width), jnp.bfloat16),
            pltpu.VMEM((rows, 128), jnp.float32),
            pltpu.VMEM((rows, 128), jnp.float32),
            pltpu.VMEM((rows, 128), jnp.float32),
            pltpu.VMEM((3, width), jnp.float32),
            pltpu.SemaphoreType.DMA((12,)),
        ],
        limit=16, scalars=[text_len, text_tiles],
    )
    sems = pltpu.SemaphoreType.DMA((32,))
    flops = 2 * width * 3 * HD
    kv, w_q = call(
        pairs_body, ids, every, [normed, k_gain[None]],
        [shape((rows, 2 * span)), shape((width, span))],
        [pltpu.VMEM((width, 2 * span), jnp.bfloat16), pltpu.SemaphoreType.DMA((64,))],
        flops=2 * rows * flops, limit=16,
    )
    kv_far = send(kv, OTHER_CORE)
    q = call(
        queries_body, ids, [], [normed, w_q, q_gain[None]], shape((imgs, span)),
        flops=imgs * flops, limit=12,
    )
    w_c = call(
        join_out_body, ids, [near_c, away_c, swap_c], [], shape((width // 4, 12 * HD)),
        [sems], limit=6,
    )
    work = 4 * half * 6 * rows * HD
    keeps, others = [], []
    for r in range(2):
        att = call(
            functools.partial(attend_body, r * half), ids, [],
            [q, kv, kv_far, bias], shape((half, span)), flops=work,
            limit=10,
        )
        all_att = [att] + [turn(att, s) for s in (1, -1, 2)]
        keep, away = call(
            functools.partial(project_body, r * half), ids, [], all_att + [w_c, pick, gates],
            [shape((half, width // 8))] * 2,
            [pltpu.VMEM((half, 12 * HD), jnp.bfloat16)],
            flops=2 * half * 12 * HD * width // 4, limit=10,
        )
        keeps.append(keep)
        others.append(send(away, OTHER_CFG))
    out = shape((imgs, width // 8), jnp.float32)
    return call(
        final_body, ids, [], keeps + others + [pick], [out, out], scalars=[step_index],
        limit=10,
    )


def solution(mesh):
    in_specs = (
        P("seq", "tp"),
        P("cfg", "seq", "tp"),
        P("cfg", None, None, None),
        P("seq", "tp"),
        P(),
        P(),
        P("tp", "seq"),
        P(),
        P(),
        P(),
    )
    out_specs = (P("seq", ("cfg", "tp")), P("seq", ("cfg", "tp")))
    return jax.shard_map(inner, mesh=mesh, in_specs=in_specs, out_specs=out_specs, check_vma=False)
```
